32 devices in a mesh: replica: 16 (over z, x, core), shard: 2 (over y).
Axes of the slice: x: 2, y: 2, z: 4, core: 2. Of those that a mesh axis runs over, the one named last changes fastest.
Arguments:
- latents: bfloat16 [32, 1024, 1152], P('replica', 'shard'), may hold values from -6 to 6
- conditions: bfloat16 [32, 1152], P('replica'), may hold values from -6 to 6
- cotangent: bfloat16 [32, 1024, 1152], P('replica', 'shard'), may hold values from -6 to 6
- counts: int32 [16], P('replica'), may hold values from 1 to 2, as said below
- w_ada: bfloat16 [1152, 6912], P('shard'), may hold values from -0.1875 to 0.1875
- b_ada: bfloat16 [6912], P('shard'), may hold values from -3 to 3
- w_qkv: bfloat16 [1152, 3456], P('shard'), may hold values from -0.1875 to 0.1875
- b_qv: bfloat16 [2304], P('shard'), may hold values from -3 to 3
- w_proj: bfloat16 [1152, 1152], P('shard'), may hold values from -3.5 to 3.5
- b_proj: bfloat16 [1152], P('shard'), may hold values from -3 to 3
- w_fc1: bfloat16 [1152, 4608], P('shard'), may hold values from -0.1875 to 0.1875
- b_fc1: bfloat16 [4608], P('shard'), may hold values from -3 to 3
- w_fc2: bfloat16 [4608, 1152], P('shard'), may hold values from -0.09375 to 0.09375
- b_fc2: bfloat16 [1152], P('shard'), may hold values from -3 to 3
Outputs:
- output: bfloat16 [32, 1024, 1152], P('replica', 'shard')
- grad_latents: float32 [32, 1024, 1152], P('replica', 'shard')
- grad_conditions: float32 [32, 1152], P('replica')
- grad_w_ada: float32 [1152, 6912], P('shard')
- grad_b_ada: float32 [6912], P('shard')
- grad_w_qkv: float32 [1152, 3456], P('shard')
- grad_b_qv: float32 [2304], P('shard')
- grad_w_proj: float32 [1152, 1152], P('shard')
- grad_b_proj: float32 [1152], P('shard')
- grad_w_fc1: float32 [1152, 4608], P('shard')
- grad_b_fc1: float32 [4608], P('shard')
- grad_w_fc2: float32 [4608, 1152], P('shard')
- grad_b_fc2: float32 [1152], P('shard')
The draws below stay inside these ranges and needn't reach their ends.
Inputs may be any that keep to these rules, and one draw needn't show every extreme that they name: counts[r] live slots on replica r are its slots 0 to counts[r] - 1 of 2; some replica has all 2 live.
All inputs are finite; a program needn't handle non-finite values.
Results may differ from the reference program's by a relative error of at most 0.019.
Values may be sent and summed in bfloat16 or wider, within the bound.
A program may use at most 512 MiB of HBM per device.

```python
import math
import jax
import jax.numpy as jnp
from jax import lax

D = 1152
HEADS = 16
HDIM = 72
FF = 4608
SEQ = 1024
SLOTS = 2
LATENTS = 32
N_REPLICA = 16


def draw_counts(key, part):
    first_key, second_key = jax.random.split(jax.random.fold_in(key, 11))
    drawn = jax.random.randint(first_key, (N_REPLICA,), 1, SLOTS + 1, dtype=jnp.int32)
    position = jax.random.randint(second_key, (), 0, N_REPLICA, dtype=jnp.int32)
    return drawn.at[position].set(SLOTS)


def shard_levels(rng, extent, shards, low, largest):
    def one(dim, blocks):
        steps = jax.random.uniform(jax.random.fold_in(jax.random.fold_in(rng, 6), dim), (blocks,), jnp.float32, low / len(shards), largest / len(shards))
        return jnp.repeat(jnp.exp(steps), extent[dim] // blocks).reshape((-1,) + (1,) * (len(extent) - dim - 1))

    gain = one(*shards[0])
    for cut in shards[1:]:
        gain = gain * one(*cut)
    return gain


def centred(rng, shape, width, bound, pieces=(), held_as=jnp.bfloat16):
    values = width * jax.random.normal(rng, shape, jnp.float32)
    if pieces:
        values = values * shard_levels(rng, shape, pieces, -0.22, 0.18)
    return jnp.clip(values, -bound, bound).astype(held_as)


def setup_inputs(seed: int = 0) -> dict:
    seeds = jax.random.split(jax.random.key(seed), 15)
    return {
        "latents": centred(seeds[0], (LATENTS, SEQ, D), 1.0, 6.0, ((0, 16), (1, 2))),
        "conditions": centred(seeds[1], (LATENTS, D), 1.0, 6.0, ((0, 16),)),
        "cotangent": centred(seeds[2], (LATENTS, SEQ, D), 1.0, 6.0, ((0, 16), (1, 2))),
        "counts": draw_counts(jax.random.fold_in(seeds[14], 71), 0),
        "w_ada": centred(seeds[4], (D, 6 * D), D ** -0.5, 0.1875, ((0, 2),)),
        "b_ada": centred(seeds[5], (6 * D,), 0.5, 3.0, ((0, 2),)),
        "w_qkv": centred(seeds[6], (D, 3 * D), D ** -0.5, 0.1875, ((0, 2),)),
        "b_qv": centred(seeds[7], (2 * D,), 0.5, 3.0, ((0, 2),)),
        "w_proj": centred(seeds[8], (D, D), (max(1, 3 * D // SEQ)) ** -0.5, 3.5, ((0, 2),)),
        "b_proj": centred(seeds[9], (D,), 0.5, 3.0, ((0, 2),)),
        "w_fc1": centred(seeds[10], (D, FF), D ** -0.5, 0.1875, ((0, 2),)),
        "b_fc1": centred(seeds[11], (FF,), 0.5, 3.0, ((0, 2),)),
        "w_fc2": centred(seeds[12], (FF, D), FF ** -0.5, 0.09375, ((0, 2),)),
        "b_fc2": centred(seeds[13], (D,), 0.5, 3.0, ((0, 2),)),
    }


@jax.custom_vjp
def low(v):
    return lax.optimization_barrier(v.astype(jnp.bfloat16)).astype(jnp.float32)

@jax.custom_vjp
def low_back(v):
    return v

def low_keep(v):
    return (low(v), None)

def low_pass(kept, grad):
    return (grad,)

def back_keep(v):
    return (v, None)

def back_low(kept, grad):
    return (low(grad),)
low.defvjp(low_keep, low_pass)
low_back.defvjp(back_keep, back_low)

def matmul_high(left, right):
    return jnp.dot(left, right, precision=lax.Precision.HIGHEST)

def normalize(values):
    centered = values - lax.optimization_barrier(jnp.mean(values, axis=-1, keepdims=True))
    return centered * lax.rsqrt(lax.optimization_barrier(jnp.mean(centered * centered, axis=-1, keepdims=True)) + 1e-06)

def layer_one(params, tokens, condition):
    w_ada, b_ada, w_qkv, b_qv, w_proj, b_proj, w_fc1, b_fc1, w_fc2, b_fc2 = params
    cond_act = low(jax.nn.silu(condition))
    modul = low_back(matmul_high(cond_act[None, :], w_ada)[0] + b_ada)
    shift_a, scale_a, gate_a, shift_m, scale_m, gate_m = jnp.split(modul, 6)
    normed = low(normalize(tokens) * (1.0 + scale_a) + shift_a)
    qkv = matmul_high(normed, w_qkv)
    query = low(low_back(qkv[:, :D] + b_qv[:D]))
    keys = low(low_back(qkv[:, D:2 * D]))
    values = low(low_back(qkv[:, 2 * D:] + b_qv[D:]))
    length = tokens.shape[0]
    query_h = query.reshape(length, HEADS, HDIM)
    keys_h = keys.reshape(length, HEADS, HDIM)
    values_h = values.reshape(length, HEADS, HDIM)
    scores = low_back(jnp.einsum('qhd,khd->hqk', query_h, keys_h, precision=lax.Precision.HIGHEST) * (1.0 / math.sqrt(HDIM)))
    probs = low(jax.nn.softmax(scores, axis=-1))
    attended = jnp.einsum('hqk,khd->qhd', probs, values_h, precision=lax.Precision.HIGHEST).reshape(length, D)
    attended = low(low_back(attended))
    branch_a = low_back(matmul_high(attended, w_proj) + b_proj)
    resid = tokens + gate_a * branch_a
    mixed = low(normalize(resid) * (1.0 + scale_m) + shift_m)
    pre = low_back(matmul_high(mixed, w_fc1) + b_fc1)
    hidden = low(jax.nn.gelu(pre, approximate=True))
    branch_m = low_back(matmul_high(hidden, w_fc2) + b_fc2)
    return resid + gate_m * branch_m

def reference(latents, conditions, cotangent, counts, w_ada, b_ada, w_qkv, b_qv, w_proj, b_proj, w_fc1, b_fc1, w_fc2, b_fc2):
    params = tuple((p.astype(jnp.float32) for p in (w_ada, b_ada, w_qkv, b_qv, w_proj, b_proj, w_fc1, b_fc1, w_fc2, b_fc2)))
    slot_ids = jnp.arange(LATENTS, dtype=jnp.int32)
    live = (slot_ids % SLOTS < counts[slot_ids // SLOTS]).astype(jnp.float32)[:, None, None]
    stepper = jax.checkpoint(layer_one)

    def forward(weights, tokens, conds):

        def turn(carried, item):
            return (carried, stepper(weights, item[0], item[1]))
        _, result = lax.scan(turn, jnp.float32(0.0), (tokens, conds))
        return result
    final, pullback = jax.vjp(forward, params, latents.astype(jnp.float32), conditions.astype(jnp.float32))
    grads, grad_latents, grad_conditions = pullback(cotangent.astype(jnp.float32) * live)
    output = (final * live).astype(jnp.bfloat16)
    return (output, grad_latents, grad_conditions, grads[0], grads[1], grads[2], grads[3], grads[4], grads[5], grads[6], grads[7], grads[8], grads[9])
```

```python
from functools import partial
import math

import jax
import jax.numpy as jnp
from jax import lax
from jax.sharding import PartitionSpec as P

HEADS = 16
HDIM = 72


epsilon = 1e-06


def layer_stats(values):
    centered = values - jnp.mean(values, axis=-1, keepdims=True)
    inverse = lax.rsqrt(jnp.mean(centered * centered, axis=-1, keepdims=True) + epsilon)
    return (centered * inverse, inverse)


def layer_back(normal, inverse, d_normal):
    first_mean = jnp.mean(d_normal, axis=-1, keepdims=True)
    second_mean = jnp.mean(d_normal * normal, axis=-1, keepdims=True)
    return inverse * (d_normal - first_mean - normal * second_mean)


def contract_last(left, right):
    return lax.dot_general(
        left, right, (((1,), (1,)), ((), ())), preferred_element_type=jnp.float32
    )


def forward_product(inputs, whole_pair):
    return (
        jnp.dot(inputs, whole_pair[0], preferred_element_type=jnp.float32),
        whole_pair[1].astype(jnp.float32),
    )


def backward_product(grads, whole_pair):
    return contract_last(grads, whole_pair[0])


def swap_cores(values):
    return lax.ppermute(values, "core", [(0, 1), (1, 0)])


def join_cores(mine, axis):
    theirs = swap_cores(mine)
    first = lax.axis_index("core") == 0
    return jnp.stack(
        [jnp.where(first, mine, theirs), jnp.where(first, theirs, mine)], axis=axis
    )


def gather_rows(weight):
    rows, columns = weight.shape
    cores = lax.axis_size("core")
    part = rows // cores
    mine = lax.dynamic_slice_in_dim(weight, lax.axis_index("core") * part, part, 0)
    pieces = lax.all_gather(mine, "shard", axis=0, tiled=False)
    whole = join_cores(pieces, 1)
    return whole.reshape(rows * lax.axis_size("shard"), columns)


def weight_grad(inputs, grads, after):
    n_shard, n_core = (lax.axis_size("shard"), lax.axis_size("core"))
    terms = lax.dot_general(
        inputs, grads, (((0,), (0,)), ((), ())), preferred_element_type=jnp.float32
    ).astype(jnp.bfloat16)
    rows, columns = terms.shape
    part = rows // (n_shard * n_core)
    terms = terms.reshape(n_shard, n_core, part, columns)
    core = lax.axis_index("core")
    keep = lax.dynamic_index_in_dim(terms, core, 1, keepdims=False)
    send = lax.dynamic_index_in_dim(terms, 1 - core, 1, keepdims=False)
    terms = (keep.astype(jnp.float32) + swap_cores(send).astype(jnp.float32)).astype(jnp.bfloat16)
    terms = lax.psum_scatter(terms, "shard", scatter_dimension=0, tiled=True)
    terms = terms.reshape(part, columns)
    if after is not None:
        terms, _ = lax.optimization_barrier((terms, after))
    total = lax.psum(terms, "chip")
    return total


def finish_grad(total):
    joined = join_cores(total, 0).astype(jnp.float32)
    return joined.reshape(2 * total.shape[0], total.shape[1])


def shards(
    latents,
    conditions,
    cotangent,
    counts,
    w_ada,
    b_ada,
    w_qkv,
    b_qv,
    w_proj,
    b_proj,
    w_fc1,
    b_fc1,
    w_fc2,
    b_fc2,
):
    slots, block, width = latents.shape
    n_rows = slots * block
    scale = 1.0 / math.sqrt(HDIM)
    live = (jnp.arange(slots, dtype=jnp.int32) < counts[0]).astype(jnp.float32)[:, None, None]
    index = lax.axis_index("shard")
    biases = (b_ada, b_qv, b_proj, b_fc1, b_fc2)
    bias_all = lax.all_gather(jnp.concatenate(biases), "shard", axis=0, tiled=False)
    full_bias = []
    start = 0
    for bias in biases:
        size = bias.shape[0]
        full_bias.append(bias_all[:, start : start + size].reshape(-1))
        start += size
    full_qkv = (gather_rows(w_qkv), full_bias[1])
    full_proj = (gather_rows(w_proj), full_bias[2])
    full_fc1 = (gather_rows(w_fc1), full_bias[3])
    full_fc2 = (gather_rows(w_fc2), full_bias[4])
    cond_float = conditions.astype(jnp.float32)
    cond_act = jax.nn.silu(cond_float).astype(jnp.bfloat16)
    ada_rows = w_ada.shape[0]
    ada_length = b_ada.shape[0]
    own_cond = lax.dynamic_slice_in_dim(cond_act, index * ada_rows, ada_rows, 1)
    ada_part = jnp.dot(own_cond, w_ada, preferred_element_type=jnp.float32)
    modul = lax.psum(ada_part, "shard") + full_bias[0].astype(jnp.float32)
    shift_a, scale_a, gate_a, shift_m, scale_m, gate_m = [
        piece[:, None, :] for piece in jnp.split(modul, 6, axis=1)
    ]
    tokens = latents.astype(jnp.float32)
    norm_a, inv_a = layer_stats(tokens)
    normed = (norm_a * (1.0 + scale_a) + shift_a).astype(jnp.bfloat16).reshape(n_rows, width)
    qkv_prod, qv_bias = forward_product(normed, full_qkv)
    query = (
        (qkv_prod[:, :width] + qv_bias[:width])
        .astype(jnp.bfloat16)
        .reshape(slots, block, HEADS, HDIM)
    )
    keys_own = qkv_prod[:, width : 2 * width].astype(jnp.bfloat16).reshape(slots, block, width)
    values_own = (
        (qkv_prod[:, 2 * width :] + qv_bias[width:])
        .astype(jnp.bfloat16)
        .reshape(slots, block, width)
    )
    keys_all, values_all = (
        lax.all_gather(keys_own, "shard", axis=1, tiled=True),
        lax.all_gather(values_own, "shard", axis=1, tiled=True),
    )
    length = keys_all.shape[1]
    keys_h = keys_all.reshape(slots, length, HEADS, HDIM)
    values_h = values_all.reshape(slots, length, HEADS, HDIM)
    scores = (
        jnp.einsum("sqhd,skhd->shqk", query, keys_h, preferred_element_type=jnp.float32) * scale
    )
    top_score = jnp.max(scores, axis=-1, keepdims=True)
    log_total = top_score + jnp.log(jnp.sum(jnp.exp(scores - top_score), axis=-1, keepdims=True))
    probs_low = jnp.exp(scores - log_total).astype(jnp.bfloat16)
    attended = jnp.einsum(
        "shqk,skhd->sqhd", probs_low, values_h, preferred_element_type=jnp.float32
    )
    attended_wide = attended
    attended = attended.astype(jnp.bfloat16).reshape(n_rows, width)
    proj_prod, proj_bias = forward_product(attended, full_proj)
    branch_a = (proj_prod + proj_bias).reshape(slots, block, width)
    resid = tokens + gate_a * branch_a
    norm_m, inv_m = layer_stats(resid)
    mixed = (norm_m * (1.0 + scale_m) + shift_m).astype(jnp.bfloat16).reshape(n_rows, width)
    fc1_prod, fc1_bias = forward_product(mixed, full_fc1)
    activated, gelu_back = jax.vjp(partial(jax.nn.gelu, approximate=True), fc1_prod + fc1_bias)
    hidden = activated.astype(jnp.bfloat16)
    fc2_prod, fc2_bias = forward_product(hidden, full_fc2)
    branch_m = (fc2_prod + fc2_bias).reshape(slots, block, width)
    final = resid + gate_m * branch_m
    output = (final * live).astype(jnp.bfloat16)
    d_out = cotangent.astype(jnp.float32) * live
    d_gate_m = jnp.sum(d_out * branch_m, axis=1)
    d_branch_m = (gate_m * d_out).astype(jnp.bfloat16).reshape(n_rows, width)
    sum_fc2 = weight_grad(hidden, d_branch_m, None)
    bias_fc2 = jnp.sum(d_branch_m, axis=0, dtype=jnp.float32)
    d_hidden = backward_product(d_branch_m, full_fc2)
    d_pre = gelu_back(d_hidden)[0].astype(jnp.bfloat16)
    sum_fc1 = weight_grad(mixed, d_pre, sum_fc2)
    bias_fc1 = jnp.sum(d_pre, axis=0, dtype=jnp.float32)
    d_mixed = backward_product(d_pre, full_fc1).reshape(slots, block, width)
    d_shift_m = jnp.sum(d_mixed, axis=1)
    d_scale_m = jnp.sum(d_mixed * norm_m, axis=1)
    d_resid = d_out + layer_back(norm_m, inv_m, d_mixed * (1.0 + scale_m))
    d_gate_a = jnp.sum(d_resid * branch_a, axis=1)
    d_branch_a = (gate_a * d_resid).astype(jnp.bfloat16).reshape(n_rows, width)
    sum_proj = weight_grad(attended, d_branch_a, sum_fc1)
    bias_proj = jnp.sum(d_branch_a, axis=0, dtype=jnp.float32)
    d_attended = (
        backward_product(d_branch_a, full_proj)
        .astype(jnp.bfloat16)
        .reshape(slots, block, HEADS, HDIM)
    )
    scores = (
        jnp.einsum("sqhd,skhd->shqk", query, keys_h, preferred_element_type=jnp.float32) * scale
    )
    probs = jnp.exp(scores - log_total)
    d_probs = jnp.einsum(
        "sqhd,skhd->shqk", d_attended, values_h, preferred_element_type=jnp.float32
    )
    inner = jnp.sum(d_attended.astype(jnp.float32) * attended_wide, axis=-1)
    inner = jnp.swapaxes(inner, 1, 2)[..., None]
    d_scores = (probs * (d_probs - inner)).astype(jnp.bfloat16)
    d_query = (
        (
            jnp.einsum("shqk,skhd->sqhd", d_scores, keys_h, preferred_element_type=jnp.float32)
            * scale
        )
        .astype(jnp.bfloat16)
        .reshape(n_rows, width)
    )
    key_terms = (
        jnp.einsum("shqk,sqhd->skhd", d_scores, query, preferred_element_type=jnp.float32).reshape(
            slots, length, width
        )
        * scale
    )
    value_terms = jnp.einsum(
        "shqk,sqhd->skhd",
        probs.astype(jnp.bfloat16),
        d_attended,
        preferred_element_type=jnp.float32,
    ).reshape(slots, length, width)
    d_keys, d_values = (
        lax.psum_scatter(
            key_terms.astype(jnp.bfloat16), "shard", scatter_dimension=1, tiled=True
        ).astype(jnp.float32),
        lax.psum_scatter(
            value_terms.astype(jnp.bfloat16), "shard", scatter_dimension=1, tiled=True
        ).astype(jnp.float32),
    )
    d_keys = d_keys.astype(jnp.bfloat16).reshape(n_rows, width)
    d_values = d_values.astype(jnp.bfloat16).reshape(n_rows, width)
    d_qkv = jnp.concatenate([d_query, d_keys, d_values], axis=1)
    qv_terms = jnp.concatenate(
        [jnp.sum(d_query, axis=0, dtype=jnp.float32), jnp.sum(d_values, axis=0, dtype=jnp.float32)]
    )
    sum_qkv = weight_grad(normed, d_qkv, sum_proj)
    d_normed = backward_product(d_qkv, full_qkv).reshape(slots, block, width)
    d_shift_a = jnp.sum(d_normed, axis=1)
    d_scale_a = jnp.sum(d_normed * norm_a, axis=1)
    grad_latents = d_resid + layer_back(norm_a, inv_a, d_normed * (1.0 + scale_a))
    d_modul_part = jnp.concatenate(
        [d_shift_a, d_scale_a, d_gate_a, d_shift_m, d_scale_m, d_gate_m], axis=1
    )
    d_modul = lax.psum(d_modul_part, "shard").astype(jnp.bfloat16)
    cond_all = lax.all_gather(own_cond, ("chip", "core"), axis=0, tiled=True)
    d_modul_all = lax.all_gather(d_modul, ("chip", "core"), axis=0, tiled=True)
    grad_w_ada = lax.dot_general(
        cond_all, d_modul_all, (((0,), (0,)), ((), ())), preferred_element_type=jnp.float32
    )
    grad_b_ada = lax.dynamic_slice_in_dim(
        jnp.sum(d_modul_all, axis=0, dtype=jnp.float32), index * ada_length, ada_length, 0
    )
    d_cond_act = lax.all_gather(contract_last(d_modul, w_ada), "shard", axis=1, tiled=True)
    _, silu_back = jax.vjp(jax.nn.silu, cond_float)
    grad_conditions = silu_back(d_cond_act)[0]
    bias_terms = lax.psum(
        jnp.concatenate([qv_terms, bias_proj, bias_fc1, bias_fc2]), ("chip", "core", "shard")
    )
    bias_grads = []
    start = 0
    for bias in biases[1:]:
        size = bias.shape[0]
        bias_grads.append(
            lax.dynamic_slice_in_dim(bias_terms, start + index * size, size, 0)
        )
        start += size * lax.axis_size("shard")
    return (
        output,
        grad_latents,
        grad_conditions,
        grad_w_ada,
        grad_b_ada,
        finish_grad(sum_qkv),
        bias_grads[0],
        finish_grad(sum_proj),
        bias_grads[1],
        finish_grad(sum_fc1),
        bias_grads[2],
        finish_grad(sum_fc2),
        bias_grads[3],
    )


def solution(mesh):
    names = mesh.axis_names
    n_replica, n_shard = (mesh.shape["replica"], mesh.shape["shard"])
    devices = mesh.devices.transpose(names.index("replica"), names.index("shard"))
    fine = jax.sharding.Mesh(
        devices.reshape(n_replica // 2, 2, n_shard), ("chip", "core", "shard")
    )
    placed = (
        P(("chip", "core"), "shard", None),
        P(("chip", "core"), None),
        P(("chip", "core"), "shard", None),
        P(("chip", "core")),
        P("shard", None),
        P("shard"),
        P("shard", None),
        P("shard"),
        P("shard", None),
        P("shard"),
        P("shard", None),
        P("shard"),
        P("shard", None),
        P("shard"),
    )
    return jax.shard_map(
        shards,
        mesh=fine,
        in_specs=placed,
        out_specs=(
            P(("chip", "core"), "shard", None),
            P(("chip", "core"), "shard", None),
            P(("chip", "core"), None),
            P("shard", None),
            P("shard"),
            P("shard", None),
            P("shard"),
            P("shard", None),
            P("shard"),
            P("shard", None),
            P("shard"),
            P("shard", None),
            P("shard"),
        ),
        check_vma=False,
    )
```
